32 devices in a mesh: band: 2 (over x), tm: 2 (over core), inp: 8 (over z, y).
Axes of the slice: x: 2, y: 2, z: 4, core: 2. Of those that a mesh axis runs over, the one named last changes fastest.
Arguments:
- samples: int32 [1024, 131072], P('inp', ('band', 'tm')), parts along dimension 1, may hold values from -128 to 127
- flags: int32 [2048], P(('band', 'inp')), parts along dimension 0, may hold values 0 or 1
Outputs:
- visibilities: bfloat16 [256, 2, 1024, 1024], P(('band', 'inp'), None, None, 'tm'), parts along dimension 0
The draws below stay inside these ranges and needn't reach their ends.
There are 2 independent parts, one for each index of `band`. The reference program is written for one: setup_inputs(seed, part) draws one part's arguments, and reference() takes and returns one part's arrays. A program takes and returns all parts, laid end to end along the dimension named above; each array names one. Nothing has to cross between parts.
Inputs may be any that keep to these rules, and one draw needn't show every extreme that they name: `samples`: whole numbers.
All inputs are finite; a program needn't handle non-finite values. No bound on the sum of `flags` on one device may be relied on, other than what follows from the above.
Results may differ from the reference program's by a relative error of at most 0.0056.
Values may be sent and summed in bfloat16 or wider, within the bound.
A program may use at most 128 MiB of HBM per device.

```python
import math
import jax
import jax.numpy as jnp
from jax import lax

NIN = 1024
NFFT = 1024
TAPS = 4
CH_FIRST = 384
CH = 128
NFR = 64
NT = 65536


def set_ends(entries, rng, smallest, high):
    longest = entries.shape.index(max(entries.shape))
    spots = []
    for shift in (0, 1):
        where = [jax.random.randint(jax.random.fold_in(rng, axis), (), 0, length) for axis, length in enumerate(entries.shape)]
        where[longest] = (where[longest] + shift) % entries.shape[longest]
        spots.append(tuple(where))
    return entries.at[spots[0]].set(smallest).at[spots[1]].set(high)


def setup_inputs(seed: int = 0, part: int = 0) -> dict:
    arg_keys = jax.random.split(jax.random.key(seed), 3)
    part_keys = jax.random.split(jax.random.fold_in(arg_keys[2], part), 3)
    samples = set_ends(jax.random.randint(part_keys[0], (NIN, NT), -128, 128), jax.random.fold_in(part_keys[0], 1), -128, 127).astype(jnp.int32)
    flags = set_ends((jax.random.randint(part_keys[1], (NIN,), 0, 8) < 7).astype(jnp.int32), jax.random.fold_in(part_keys[1], 1), 0, 1)
    return dict(samples=samples, flags=flags)


def window_table():
    positions = jnp.arange(TAPS * NFFT, dtype=jnp.float32) + 0.5
    shaped = jnp.sinc((positions - TAPS * NFFT / 2) / NFFT)
    taper = 0.5 - 0.5 * jnp.cos(2 * math.pi * positions / (TAPS * NFFT))
    return (shaped * taper).reshape(TAPS, NFFT)

def transform_table():
    sample_idx = jnp.arange(NFFT, dtype=jnp.int32)
    chan_idx = CH_FIRST + jnp.arange(CH, dtype=jnp.int32)
    angles = (sample_idx[:, None] * chan_idx[None, :] % NFFT).astype(jnp.float32) * (2 * math.pi / NFFT)
    both = jnp.stack([jnp.cos(angles), -jnp.sin(angles)], axis=1) / math.sqrt(NFFT)
    return both.reshape(NFFT, 2 * CH)

def filter_bank(extended, window, frames):
    summed = jnp.zeros((extended.shape[0], frames, NFFT), jnp.float32)
    for tap_index in range(TAPS):
        begin = TAPS - 1 - tap_index
        summed = summed + window[tap_index] * extended[:, begin:begin + frames]
    return summed

def transform(filtered, table):
    rows, frames, width = filtered.shape
    out = jnp.dot(filtered.reshape(rows * frames, width), table, precision=lax.Precision.HIGHEST, preferred_element_type=jnp.float32)
    return out.reshape(rows, frames, 2, CH)

def correlate_single(block):
    left_side = block.astype(jnp.float32)
    depth = 2 * left_side.shape[0]
    real_rows = left_side.reshape(depth, NIN)
    imag_rows = jnp.stack([left_side[:, 1], -left_side[:, 0]], axis=1).reshape(depth, NIN)
    left_both = jnp.stack([real_rows, imag_rows])
    out = jnp.einsum('rka,kb->rab', left_both, real_rows, precision=lax.Precision.HIGHEST)
    return out.astype(jnp.bfloat16)

def reference(samples, flags):
    voltage = (samples.astype(jnp.float32) / 128.0).astype(jnp.bfloat16)
    values = voltage.astype(jnp.float32).reshape(NIN, NFR, NFFT)
    leading = jnp.zeros((NIN, TAPS - 1, NFFT), jnp.float32)
    extended = jnp.concatenate([leading, values], axis=1)
    filtered = filter_bank(extended, window_table(), NFR)
    spectra = transform(filtered, transform_table())
    weight = flags.astype(jnp.float32)[:, None, None, None]
    channels = (spectra * weight).astype(jnp.bfloat16).transpose(3, 1, 2, 0)
    return lax.map(correlate_single, channels)
```

```python
import functools
import math

import jax
import jax.numpy as jnp
import ml_dtypes
import numpy as np
from jax import lax
from jax.experimental import pallas as pl
from jax.experimental.pallas import tpu as pltpu
from jax.sharding import PartitionSpec as P

NFFT = 1024
TAPS = 4
CH_FIRST = 384
CH = 128
CHUNK = 16
MESH = pl.DeviceIdType.MESH


def window_table():
    positions = np.arange(TAPS * NFFT, dtype=np.float64) + 0.5
    shaped = np.sinc((positions - TAPS * NFFT / 2) / NFFT)
    taper = 0.5 - 0.5 * np.cos(2 * math.pi * positions / (TAPS * NFFT))
    return (shaped * taper).reshape(TAPS, NFFT)


def transform_table():
    sample_idx = np.arange(NFFT)
    chan_idx = CH_FIRST + np.arange(CH)
    angles = (chan_idx[:, None] * sample_idx[None, :] % NFFT) * (2 * math.pi / NFFT)
    both = np.stack([np.cos(angles), -np.sin(angles)], axis=1) / math.sqrt(NFFT)
    return both.reshape(2 * CH, NFFT)


def split_table():
    table = transform_table().astype(np.float32)
    high = table.astype(ml_dtypes.bfloat16)
    low = (table - high.astype(np.float32)).astype(ml_dtypes.bfloat16)
    return np.concatenate([high, low], axis=0)


def spread_kernel(
    peers, frames, samples, flags, window, table, gathered,
    volts, halo_out, halo_in, high, low, spectra, ready,
    load_sem, halo_sems, send_sem, recv_sem, fwd_send, fwd_recv, own_sem,
):
    rows = samples.shape[0]
    lead = TAPS - 1
    chunks = frames // CHUNK
    me = lax.axis_index("inp")
    core = lax.axis_index("tm")
    other = 1 - core
    mine = ready.shape[1] // peers
    offsets = sorted(range(1, peers), key=lambda d: (abs(d - peers / 2), d))

    def load(frame):
        return pltpu.make_async_copy(
            samples.at[:, pl.ds(pl.multiple_of(frame * NFFT, NFFT), NFFT)],
            volts.at[frame + lead],
            load_sem.at[frame],
        )

    order = list(range(frames - lead, frames))
    for chunk in reversed(range(chunks)):
        begin = max(0, chunk * CHUNK - lead)
        order += [f for f in range(begin, (chunk + 1) * CHUNK) if f not in order]
    for frame in order:
        load(frame).start()

    barrier = pltpu.get_barrier_semaphore()
    for d in offsets:
        pl.semaphore_signal(
            barrier, inc=1, device_id={"inp": lax.rem(me + d, peers)}, device_id_type=MESH
        )
    pl.semaphore_signal(barrier, inc=1, device_id={"tm": other}, device_id_type=MESH)
    pl.semaphore_wait(barrier, peers)

    halo = pltpu.make_async_remote_copy(
        src_ref=halo_out, dst_ref=halo_in, send_sem=halo_sems.at[0], recv_sem=halo_sems.at[1],
        device_id={"tm": other}, device_id_type=MESH,
    )
    for j in range(lead):
        load(frames - lead + j).wait()
        halo_out[j] = volts[frames + j].astype(jnp.float32).astype(jnp.bfloat16)
    halo.start()

    def filter_pair(first):
        def row_group(g, carry):
            at = pl.ds(pl.multiple_of(g * 16, 16), 16)
            for part in range(NFFT // 256):
                cols = slice(part * 256, (part + 1) * 256)
                values = [
                    volts[first + j, at, cols].astype(jnp.float32) for j in range(TAPS + 1)
                ]
                taps = [
                    jnp.broadcast_to(window[k : k + 1, cols], (16, 256)) for k in range(TAPS)
                ]
                for j in range(2):
                    total = taps[0] * values[lead + j]
                    for k in range(1, TAPS):
                        total = total + taps[k] * values[lead + j - k]
                    top = total.astype(jnp.bfloat16)
                    dest = pl.ds(pl.multiple_of(j * rows + g * 16, 16), 16)
                    high[dest, cols] = top
                    low[dest, cols] = (total - top.astype(jnp.float32)).astype(jnp.bfloat16)
            return carry

        lax.fori_loop(0, rows // 16, row_group, 0)

    dims = (((1,), (1,)), ((), ()))

    def compute(chunk):
        def pair(q, carry):
            first = chunk * CHUNK + 2 * q
            filter_pair(first)
            both = lax.dot_general(
                table[...], high[...], dims, preferred_element_type=jnp.float32
            )
            rest = lax.dot_general(
                table[: 2 * CH], low[...], dims, preferred_element_type=jnp.float32
            )
            total = both[: 2 * CH] + (both[2 * CH :] + rest)
            good = flags[0:1, :]
            for j in range(2):
                spectra[pl.ds(pl.multiple_of((2 * q + j) * 2 * CH, 2 * CH), 2 * CH), :] = (
                    total[:, j * rows : (j + 1) * rows] * good
                )
            return carry

        lax.fori_loop(0, CHUNK // 2, pair, 0)

        def regroup(step, carry):
            for u in range(8):
                r = step * 8 + u
                ready[chunk, r] = spectra[pl.ds(r, CHUNK, stride=2 * CH), :].astype(
                    jnp.bfloat16
                )
            return carry

        lax.fori_loop(0, 2 * CH // 8, regroup, 0)

    def to_peer(chunk, d):
        dest = lax.rem(me + d, peers)
        return pltpu.make_async_remote_copy(
            src_ref=ready.at[chunk, pl.ds(dest * mine, mine)],
            dst_ref=gathered.at[me, core, chunk],
            send_sem=send_sem.at[chunk, d], recv_sem=recv_sem.at[chunk, d],
            device_id={"inp": dest}, device_id_type=MESH,
        )

    def own_local(chunk):
        return pltpu.make_async_copy(
            ready.at[chunk, pl.ds(me * mine, mine)], gathered.at[me, core, chunk],
            own_sem.at[chunk],
        )

    def own_other(chunk):
        return pltpu.make_async_remote_copy(
            src_ref=ready.at[chunk, pl.ds(me * mine, mine)],
            dst_ref=gathered.at[me, core, chunk],
            send_sem=fwd_send.at[chunk, 0], recv_sem=fwd_recv.at[chunk, 0],
            device_id={"tm": other}, device_id_type=MESH,
        )

    def forward(chunk, d):
        src = lax.rem(me + peers - d, peers)
        block = gathered.at[src, core, chunk]
        return pltpu.make_async_remote_copy(
            src_ref=block, dst_ref=block,
            send_sem=fwd_send.at[chunk, d], recv_sem=fwd_recv.at[chunk, d],
            device_id={"tm": other}, device_id_type=MESH,
        )

    waited = set(range(frames - lead, frames))
    for chunk in reversed(range(chunks)):
        for f in range(max(0, chunk * CHUNK - lead), (chunk + 1) * CHUNK):
            if f not in waited:
                waited.add(f)
                load(f).wait()
        if chunk == 0:
            halo.wait()
            scale = core.astype(jnp.float32)
            for j in range(lead):
                volts[j] = (halo_in[j].astype(jnp.float32) * scale).astype(jnp.int32)
        compute(chunk)
        for d in offsets:
            to_peer(chunk, d).start()
        own_local(chunk).start()
        own_other(chunk).start()

    for chunk in reversed(range(chunks)):
        for d in offsets:
            to_peer(chunk, d).wait_recv()
            forward(chunk, d).start()
    for chunk in reversed(range(chunks)):
        own_local(chunk).wait()
        own_other(chunk).wait()
        for d in offsets:
            to_peer(chunk, d).wait_send()
            forward(chunk, d).wait()


def spread(samples, flags, peers):
    rows, width = samples.shape
    frames = width // NFFT
    chunks = frames // CHUNK
    lead = TAPS - 1
    window = jnp.asarray((window_table() / 128.0).astype(np.float32))
    table = jnp.asarray(split_table())
    good = jnp.broadcast_to(flags.astype(jnp.float32)[None, :], (8, rows))
    vmem = pl.BlockSpec(memory_space=pltpu.VMEM)
    anywhere = pl.BlockSpec(memory_space=pl.ANY)
    return pl.pallas_call(
        functools.partial(spread_kernel, peers, frames),
        out_shape=jax.ShapeDtypeStruct(
            (peers, 2, chunks, 2 * CH // peers, CHUNK, rows), jnp.bfloat16
        ),
        in_specs=[anywhere, vmem, vmem, vmem],
        out_specs=anywhere,
        scratch_shapes=[
            pltpu.VMEM((frames + lead, rows, NFFT), jnp.int32),
            pltpu.VMEM((lead, rows, NFFT), jnp.bfloat16),
            pltpu.VMEM((lead, rows, NFFT), jnp.bfloat16),
            pltpu.VMEM((2 * rows, NFFT), jnp.bfloat16),
            pltpu.VMEM((2 * rows, NFFT), jnp.bfloat16),
            pltpu.VMEM((CHUNK * 2 * CH, rows), jnp.float32),
            pltpu.VMEM((chunks, 2 * CH, CHUNK, rows), jnp.bfloat16),
            pltpu.SemaphoreType.DMA((frames,)),
            pltpu.SemaphoreType.DMA((2,)),
            pltpu.SemaphoreType.DMA((chunks, peers)),
            pltpu.SemaphoreType.DMA((chunks, peers)),
            pltpu.SemaphoreType.DMA((chunks, peers)),
            pltpu.SemaphoreType.DMA((chunks, peers)),
            pltpu.SemaphoreType.DMA((chunks,)),
        ],
        compiler_params=pltpu.CompilerParams(
            collective_id=0, has_side_effects=True, vmem_limit_bytes=48 << 20
        ),
        name="filter_transform_spread",
    )(samples, good, window, table)


def correlate_kernel(block, out, left, right):
    peers, cores, chunks, _, length, rows = block.shape
    half = peers // 2
    core = lax.axis_index("tm")
    width = length * 2
    for src in range(peers):
        cols = slice(src * rows, (src + 1) * rows)
        for t in range(cores):
            for k in range(chunks):
                at = (t * chunks + k) * width
                real, imag = block[src, t, k, 0], block[src, t, k, 1]
                left[0, at : at + length, cols] = real
                left[0, at + length : at + width, cols] = imag
                left[1, at : at + length, cols] = imag
                left[1, at + length : at + width, cols] = -real
    for s in range(half):
        cols = slice(s * rows, (s + 1) * rows)
        for t in range(cores):
            for k in range(chunks):
                at = (t * chunks + k) * width
                right[at : at + length, cols] = block[core * half + s, t, k, 0]
                right[at + length : at + width, cols] = block[core * half + s, t, k, 1]
    step = 256
    for r in range(2):
        for a in range(0, left.shape[2], step):
            out[0, r, a : a + step, :] = lax.dot_general(
                left[r, :, a : a + step], right[...], (((0,), (0,)), ((), ())),
                preferred_element_type=jnp.float32,
            ).astype(jnp.bfloat16)


def correlate_blocks(gathered):
    peers, cores, chunks, parts, length, rows = gathered.shape
    chans = parts // 2
    total = peers * rows
    depth = cores * chunks * 2 * length
    return pl.pallas_call(
        correlate_kernel,
        grid=(chans,),
        out_shape=jax.ShapeDtypeStruct((chans, 2, total, total // 2), jnp.bfloat16),
        in_specs=[
            pl.BlockSpec(
                (peers, cores, chunks, 2, length, rows), lambda c: (0, 0, 0, c, 0, 0)
            )
        ],
        out_specs=pl.BlockSpec((1, 2, total, total // 2), lambda c: (c, 0, 0, 0)),
        scratch_shapes=[
            pltpu.VMEM((2, depth, total), jnp.bfloat16),
            pltpu.VMEM((depth, total // 2), jnp.bfloat16),
        ],
        compiler_params=pltpu.CompilerParams(vmem_limit_bytes=48 << 20),
        name="correlate",
    )(gathered)


def filter_bank(extended, window, frames):
    summed = jnp.zeros((extended.shape[0], frames, NFFT), jnp.float32)
    for tap_index in range(TAPS):
        begin = TAPS - 1 - tap_index
        summed = summed + window[tap_index] * extended[:, begin : begin + frames]
    return summed


def general(samples, flags):
    rows = samples.shape[0]
    frames = samples.shape[1] // NFFT
    window = jnp.asarray(window_table().astype(np.float32))
    table = jnp.asarray(transform_table().astype(np.float32))
    voltage = (samples.astype(jnp.float32) / 128.0).astype(jnp.bfloat16)
    voltage = voltage.reshape(rows, frames, NFFT)
    received = lax.ppermute(voltage[:, frames - (TAPS - 1) :], "tm", [(0, 1)])
    extended = jnp.concatenate([received, voltage], axis=1).astype(jnp.float32)
    filtered = filter_bank(extended, window, frames)
    spectra = lax.dot_general(
        filtered.reshape(rows * frames, NFFT), table, (((1,), (1,)), ((), ())),
        precision=lax.Precision.HIGHEST, preferred_element_type=jnp.float32,
    ).reshape(rows, frames, CH, 2)
    weight = flags.astype(jnp.float32)[:, None, None, None]
    channels = (spectra * weight).astype(jnp.bfloat16).transpose(2, 1, 3, 0)
    spread_out = lax.all_to_all(channels, "inp", split_axis=0, concat_axis=3, tiled=True)
    left = lax.all_gather(spread_out, "tm", axis=1, tiled=True)
    chans, _, _, total = left.shape
    half = total // 2
    right = lax.dynamic_slice_in_dim(left, lax.axis_index("tm") * half, half, 3)
    turned = jnp.stack([left[:, :, 1], -left[:, :, 0]], axis=2)
    both = jnp.stack([left, turned], axis=1).reshape(chans, 2, -1, total)
    out = jnp.einsum(
        "crka,ckb->crab", both, right.reshape(chans, -1, half),
        preferred_element_type=jnp.float32,
    )
    return out.astype(jnp.bfloat16)


def solution(mesh):
    peers = mesh.shape["inp"]

    def local(samples, flags):
        rows, width = samples.shape
        fits = (
            rows == 128 and peers % 2 == 0 and mesh.shape["tm"] == 2
            and (width // NFFT) % CHUNK == 0 and 2 * CH % (2 * peers) == 0
        )
        if not fits:
            return general(samples, flags)
        return correlate_blocks(spread(samples, flags, peers))

    return jax.shard_map(
        local,
        mesh=mesh,
        in_specs=(P("inp", ("band", "tm")), P(("band", "inp"))),
        out_specs=P(("band", "inp"), None, None, "tm"),
        check_vma=False,
    )
```

```python
import functools
import math

import jax
import jax.numpy as jnp
import ml_dtypes
import numpy as np
from jax import lax
from jax.experimental import pallas as pl
from jax.experimental.pallas import tpu as pltpu
from jax.sharding import PartitionSpec as P

NFFT = 1024
TAPS = 4
CH_FIRST = 384
CH = 128
CHUNK = 8
MESH = pl.DeviceIdType.MESH


def window_table():
    positions = np.arange(TAPS * NFFT, dtype=np.float64) + 0.5
    shaped = np.sinc((positions - TAPS * NFFT / 2) / NFFT)
    taper = 0.5 - 0.5 * np.cos(2 * math.pi * positions / (TAPS * NFFT))
    return (shaped * taper).reshape(TAPS, NFFT)


def transform_table():
    sample_idx = np.arange(NFFT)
    chan_idx = CH_FIRST + np.arange(CH)
    angles = (chan_idx[:, None] * sample_idx[None, :] % NFFT) * (2 * math.pi / NFFT)
    both = np.stack([np.cos(angles), -np.sin(angles)], axis=1) / math.sqrt(NFFT)
    return both.reshape(2 * CH, NFFT)


def split_table():
    table = transform_table().astype(np.float32)
    high = table.astype(ml_dtypes.bfloat16)
    low = (table - high.astype(np.float32)).astype(ml_dtypes.bfloat16)
    return np.concatenate([high, low], axis=0)


def spread_kernel(
    peers, frames, samples, flags_hbm, window_hbm, table_hbm, gathered,
    volts, flags, window, table, halo_out, halo_in, high, low, spectra, ready,
    load_sem, const_sem, halo_sems, send_sem, recv_sem, fwd_send, fwd_recv, own_sem,
):
    rows = samples.shape[0]
    lead = TAPS - 1
    chunks = frames // CHUNK
    me = lax.axis_index("inp")
    core = lax.axis_index("tm")
    other = 1 - core
    mine = ready.shape[1] // peers
    offsets = sorted(range(1, peers), key=lambda d: (abs(d - peers / 2), d))

    def load(frame):
        return pltpu.make_async_copy(
            samples.at[:, pl.ds(pl.multiple_of(frame * NFFT, NFFT), NFFT)],
            volts.at[frame + lead],
            load_sem.at[frame],
        )

    def barrier_part(wait):
        barrier = pltpu.get_barrier_semaphore()
        if wait:
            pl.semaphore_wait(barrier, peers)
            return
        for d in offsets:
            pl.semaphore_signal(
                barrier, inc=1, device_id={"inp": lax.rem(me + d, peers)}, device_id_type=MESH
            )
        pl.semaphore_signal(barrier, inc=1, device_id={"tm": other}, device_id_type=MESH)

    constants = [
        pltpu.make_async_copy(src, dst, const_sem.at[k])
        for k, (src, dst) in enumerate(
            [(window_hbm, window), (flags_hbm, flags), (table_hbm, table)]
        )
    ]
    order = []
    for chunk in reversed(range(chunks)):
        begin = max(0, chunk * CHUNK - lead)
        order += [f for f in range(begin, (chunk + 1) * CHUNK) if f not in order]
    for frame in order[:5]:
        load(frame).start()
    for constant in constants:
        constant.start()
    for frame in order[5:]:
        load(frame).start()
    barrier_part(False)

    halo = pltpu.make_async_remote_copy(
        src_ref=halo_out, dst_ref=halo_in, send_sem=halo_sems.at[0], recv_sem=halo_sems.at[1],
        device_id={"tm": other}, device_id_type=MESH,
    )

    def filter_pair(first):
        def row_group(g, carry):
            at = pl.ds(pl.multiple_of(g * 16, 16), 16)
            for part in range(NFFT // 256):
                cols = slice(part * 256, (part + 1) * 256)
                values = [
                    volts[first + j, at, cols].astype(jnp.float32) for j in range(TAPS + 1)
                ]
                taps = [
                    jnp.broadcast_to(window[k : k + 1, cols], (16, 256)) for k in range(TAPS)
                ]
                for j in range(2):
                    total = taps[0] * values[lead + j]
                    for k in range(1, TAPS):
                        total = total + taps[k] * values[lead + j - k]
                    top = total.astype(jnp.bfloat16)
                    dest = pl.ds(pl.multiple_of(j * rows + g * 16, 16), 16)
                    high[dest, cols] = top
                    low[dest, cols] = (total - top.astype(jnp.float32)).astype(jnp.bfloat16)
            return carry

        lax.fori_loop(0, rows // 16, row_group, 0)

    dims = (((1,), (1,)), ((), ()))

    def compute(chunk):
        good = flags[0:1, :].astype(jnp.float32)

        def pair(q, carry):
            first = chunk * CHUNK + 2 * q
            if chunk == chunks - 1:
                load(first).wait()
                load(first + 1).wait()
            filter_pair(first)
            both = lax.dot_general(
                table[...], high[...], dims, preferred_element_type=jnp.float32
            )
            rest = lax.dot_general(
                table[: 2 * CH], low[...], dims, preferred_element_type=jnp.float32
            )
            total = both[: 2 * CH] + (both[2 * CH :] + rest)
            for j in range(2):
                spectra[pl.ds(pl.multiple_of((2 * q + j) * 2 * CH, 2 * CH), 2 * CH), :] = (
                    total[:, j * rows : (j + 1) * rows] * good
                )
            return carry

        lax.fori_loop(0, CHUNK // 2, pair, 0)

    def regroup(chunk, dest):
        unroll = math.gcd(mine, 8)

        def some(step, carry):
            for u in range(unroll):
                chan = dest * mine + step * unroll + u
                parts = [
                    spectra[pl.ds(2 * chan + p, CHUNK, stride=2 * CH), :] for p in range(2)
                ]
                ready[chunk, chan] = jnp.concatenate(parts, axis=0).astype(jnp.bfloat16)
            return carry

        lax.fori_loop(0, mine // unroll, some, 0)

    def to_peer(chunk, d):
        dest = lax.rem(me + d, peers)
        return pltpu.make_async_remote_copy(
            src_ref=ready.at[chunk, pl.ds(dest * mine, mine)],
            dst_ref=gathered.at[me, core, chunk],
            send_sem=send_sem.at[chunk, d], recv_sem=recv_sem.at[chunk, d],
            device_id={"inp": dest}, device_id_type=MESH,
        )

    def own_local(chunk):
        return pltpu.make_async_copy(
            ready.at[chunk, pl.ds(me * mine, mine)], gathered.at[me, core, chunk],
            own_sem.at[chunk],
        )

    def own_other(chunk):
        return pltpu.make_async_remote_copy(
            src_ref=ready.at[chunk, pl.ds(me * mine, mine)],
            dst_ref=gathered.at[me, core, chunk],
            send_sem=fwd_send.at[chunk, 0], recv_sem=fwd_recv.at[chunk, 0],
            device_id={"tm": other}, device_id_type=MESH,
        )

    def forward(chunk, d):
        src = lax.rem(me + peers - d, peers)
        block = gathered.at[src, core, chunk]
        return pltpu.make_async_remote_copy(
            src_ref=block, dst_ref=block,
            send_sem=fwd_send.at[chunk, d], recv_sem=fwd_recv.at[chunk, d],
            device_id={"tm": other}, device_id_type=MESH,
        )

    waited = set(range((chunks - 1) * CHUNK, frames))
    for chunk in reversed(range(chunks)):
        for f in range(max(0, chunk * CHUNK - lead), (chunk + 1) * CHUNK):
            if f not in waited:
                waited.add(f)
                load(f).wait()
        if chunk == chunks - 1:
            for constant in constants:
                constant.wait()
        if chunk == 0:
            halo.wait()
            scale = core.astype(jnp.float32)
            for j in range(lead):
                volts[j] = (halo_in[j].astype(jnp.float32) * scale).astype(jnp.int32)
        compute(chunk)
        if chunk == chunks - 1:
            barrier_part(True)
        for d in offsets:
            regroup(chunk, lax.rem(me + d, peers))
            to_peer(chunk, d).start()
        regroup(chunk, me)
        own_local(chunk).start()
        own_other(chunk).start()
        if chunk == chunks - 1:
            for j in range(lead):
                halo_out[j] = volts[frames + j].astype(jnp.float32).astype(jnp.bfloat16)
            halo.start()

    for chunk in reversed(range(chunks)):
        for d in offsets:
            to_peer(chunk, d).wait_recv()
            forward(chunk, d).start()
    for chunk in reversed(range(chunks)):
        own_local(chunk).wait()
        own_other(chunk).wait()
        for d in offsets:
            to_peer(chunk, d).wait_send()
            forward(chunk, d).wait()


def spread(samples, flags, peers):
    rows, width = samples.shape
    frames = width // NFFT
    chunks = frames // CHUNK
    lead = TAPS - 1
    window = jnp.asarray((window_table() / 128.0).astype(np.float32))
    table = jnp.asarray(split_table())
    good = flags.reshape(1, rows)
    stay = pl.BlockSpec(memory_space=pltpu.HBM)
    anywhere = pl.BlockSpec(memory_space=pl.ANY)
    return pl.pallas_call(
        functools.partial(spread_kernel, peers, frames),
        out_shape=jax.ShapeDtypeStruct(
            (peers, 2, chunks, CH // peers, 2 * CHUNK, rows), jnp.bfloat16
        ),
        in_specs=[stay, stay, stay, stay],
        out_specs=anywhere,
        scratch_shapes=[
            pltpu.VMEM((frames + lead, rows, NFFT), jnp.int32),
            pltpu.VMEM((1, rows), jnp.int32),
            pltpu.VMEM((TAPS, NFFT), jnp.float32),
            pltpu.VMEM((4 * CH, NFFT), jnp.bfloat16),
            pltpu.VMEM((lead, rows, NFFT), jnp.bfloat16),
            pltpu.VMEM((lead, rows, NFFT), jnp.bfloat16),
            pltpu.VMEM((2 * rows, NFFT), jnp.bfloat16),
            pltpu.VMEM((2 * rows, NFFT), jnp.bfloat16),
            pltpu.VMEM((CHUNK * 2 * CH, rows), jnp.float32),
            pltpu.VMEM((chunks, CH, 2 * CHUNK, rows), jnp.bfloat16),
            pltpu.SemaphoreType.DMA((frames,)),
            pltpu.SemaphoreType.DMA((3,)),
            pltpu.SemaphoreType.DMA((2,)),
            pltpu.SemaphoreType.DMA((chunks, peers)),
            pltpu.SemaphoreType.DMA((chunks, peers)),
            pltpu.SemaphoreType.DMA((chunks, peers)),
            pltpu.SemaphoreType.DMA((chunks, peers)),
            pltpu.SemaphoreType.DMA((chunks,)),
        ],
        compiler_params=pltpu.CompilerParams(
            collective_id=0, has_side_effects=True, vmem_limit_bytes=48 << 20
        ),
        name="filter_transform_spread",
    )(samples, good, window, table)


def correlate_kernel(block, out, left, right):
    peers, cores, chunks, _, length, rows = block.shape
    half = peers // 2
    frames = length // 2
    width = half * rows
    core = lax.axis_index("tm")
    for t in range(cores):
        for k in range(chunks):
            at = (t * chunks + k) * length
            for src in range(peers):
                left[at : at + length, src * rows : (src + 1) * rows] = block[src, t, k, 0]
            for s in range(half):
                tile = block[core * half + s, t, k, 0]
                wide = tile.astype(jnp.float32)
                turned = jnp.concatenate([-wide[frames:], wide[:frames]], axis=0)
                right[at : at + length, s * rows : (s + 1) * rows] = tile
                right[at : at + length, width + s * rows : width + (s + 1) * rows] = (
                    turned.astype(jnp.bfloat16)
                )
    step = 256
    for a in range(0, left.shape[1], step):
        both = lax.dot_general(
            left[:, a : a + step], right[...], (((0,), (0,)), ((), ())),
            preferred_element_type=jnp.float32,
        ).astype(jnp.bfloat16)
        out[0, 0, a : a + step, :] = both[:, :width]
        out[0, 1, a : a + step, :] = both[:, width:]


def correlate_blocks(gathered):
    peers, cores, chunks, chans, length, rows = gathered.shape
    total = peers * rows
    depth = cores * chunks * length
    return pl.pallas_call(
        correlate_kernel,
        grid=(chans,),
        out_shape=jax.ShapeDtypeStruct((chans, 2, total, total // 2), jnp.bfloat16),
        in_specs=[
            pl.BlockSpec(
                (peers, cores, chunks, 1, length, rows), lambda c: (0, 0, 0, c, 0, 0)
            )
        ],
        out_specs=pl.BlockSpec((1, 2, total, total // 2), lambda c: (c, 0, 0, 0)),
        scratch_shapes=[
            pltpu.VMEM((depth, total), jnp.bfloat16),
            pltpu.VMEM((depth, total), jnp.bfloat16),
        ],
        compiler_params=pltpu.CompilerParams(vmem_limit_bytes=48 << 20),
        name="correlate",
    )(gathered)


def filter_bank(extended, window, frames):
    summed = jnp.zeros((extended.shape[0], frames, NFFT), jnp.float32)
    for tap_index in range(TAPS):
        begin = TAPS - 1 - tap_index
        summed = summed + window[tap_index] * extended[:, begin : begin + frames]
    return summed


def general(samples, flags):
    rows = samples.shape[0]
    frames = samples.shape[1] // NFFT
    window = jnp.asarray(window_table().astype(np.float32))
    table = jnp.asarray(transform_table().astype(np.float32))
    voltage = (samples.astype(jnp.float32) / 128.0).astype(jnp.bfloat16)
    voltage = voltage.reshape(rows, frames, NFFT)
    received = lax.ppermute(voltage[:, frames - (TAPS - 1) :], "tm", [(0, 1)])
    extended = jnp.concatenate([received, voltage], axis=1).astype(jnp.float32)
    filtered = filter_bank(extended, window, frames)
    spectra = lax.dot_general(
        filtered.reshape(rows * frames, NFFT), table, (((1,), (1,)), ((), ())),
        precision=lax.Precision.HIGHEST, preferred_element_type=jnp.float32,
    ).reshape(rows, frames, CH, 2)
    weight = flags.astype(jnp.float32)[:, None, None, None]
    channels = (spectra * weight).astype(jnp.bfloat16).transpose(2, 1, 3, 0)
    spread_out = lax.all_to_all(channels, "inp", split_axis=0, concat_axis=3, tiled=True)
    left = lax.all_gather(spread_out, "tm", axis=1, tiled=True)
    chans, _, _, total = left.shape
    half = total // 2
    right = lax.dynamic_slice_in_dim(left, lax.axis_index("tm") * half, half, 3)
    turned = jnp.stack([left[:, :, 1], -left[:, :, 0]], axis=2)
    both = jnp.stack([left, turned], axis=1).reshape(chans, 2, -1, total)
    out = jnp.einsum(
        "crka,ckb->crab", both, right.reshape(chans, -1, half),
        preferred_element_type=jnp.float32,
    )
    return out.astype(jnp.bfloat16)


def solution(mesh):
    peers = mesh.shape["inp"]

    def local(samples, flags):
        rows, width = samples.shape
        fits = (
            rows == 128 and peers % 2 == 0 and mesh.shape["tm"] == 2
            and (width // NFFT) % CHUNK == 0 and 2 * CH % (2 * peers) == 0
        )
        if not fits:
            return general(samples, flags)
        return correlate_blocks(spread(samples, flags, peers))

    return jax.shard_map(
        local,
        mesh=mesh,
        in_specs=(P("inp", ("band", "tm")), P(("band", "inp"))),
        out_specs=P(("band", "inp"), None, None, "tm"),
        check_vma=False,
    )
```
